32 devices in a mesh: dp: 4 (over z), mp: 8 (over y, x, core).
Axes of the slice: x: 2, y: 2, z: 4, core: 2. Of those that a mesh axis runs over, the one named last changes fastest.
Arguments:
- behaviors: bfloat16 [32, 2048, 1024], P('dp', 'mp'), may hold values from -8 to 8
- candidates: bfloat16 [32, 2048, 128], P('dp', 'mp'), may hold values from -12 to 12
- lengths: int32 [32], P('dp'), may hold values from 128 to 1024
- bilinear: bfloat16 [2048, 2048], P('mp'), may hold values from -1 to 2
- norm_gain: float32 [2048], replicated, may hold values from 0.1 to 1.9
- w_gate: bfloat16 [2048, 8192], P('dp', 'mp'), may hold values from -0.125 to 0.125
- w_up: bfloat16 [2048, 8192], P('dp', 'mp'), may hold values from -0.125 to 0.125
- w_down: bfloat16 [8192, 2048], P('mp', 'dp'), may hold values from -0.0625 to 0.0625
Outputs:
- interest: bfloat16 [32, 2048, 128], P('dp', 'mp')
The draws below stay inside these ranges and needn't reach their ends.
All inputs are finite; a program needn't handle non-finite values.
Results may differ from the reference program's by a relative error of at most 0.015.
Values may be sent and summed in bfloat16 or wider, within the bound.
No kernel may reach another device: no remote copies, remote signals or barrier semaphores. Data moves between devices by JAX's collectives and lax.ppermute only.
A program may use at most 64 MiB of HBM per device.

```python
import math
import jax
import jax.numpy as jnp
from jax import lax

D = 2048
FF = 8192
L = 1024
C = 128
USERS = 32
N_MP = 8


def base_behaviors(key):
    first_key = jax.random.fold_in(jax.random.fold_in(key, 7), 0)
    bulk = jnp.clip(jax.random.normal(first_key, (USERS, D, L), jnp.float32), -6.0, 6.0)
    return bulk


def draw_behaviors(key, part):
    return base_behaviors(key).astype(jnp.bfloat16)


def draw_candidates(key, part):
    cand_key = jax.random.fold_in(jax.random.fold_in(key, 13), 0)
    cand = jnp.clip(jax.random.normal(cand_key, (USERS, D, C), jnp.float32), -6.0, 6.0)
    return cand.astype(jnp.bfloat16)


def draw_bilinear(key, part):
    noise = jnp.clip(jax.random.normal(jax.random.fold_in(key, 21), (D, D), jnp.float32), -6.0, 6.0)
    return (jnp.eye(D, dtype=jnp.float32) + noise * (0.7 / jnp.sqrt(jnp.float32(D)))).astype(jnp.bfloat16)


def with_ends(drawn, key, low, high):
    shape = drawn.shape
    place = [jax.random.randint(jax.random.fold_in(key, axis), (), 0, shape[axis]) for axis in range(len(shape))]
    drawn = drawn.at[tuple(place)].set(low)
    longest = shape.index(max(shape))
    place[longest] = (place[longest] + 1) % shape[longest]
    return drawn.at[tuple(place)].set(high)


def level_of(rng, extent, shards, smallest, largest):
    factor_of, own = 1.0, jax.random.fold_in(rng, 6)
    for position, blocks in shards:
        heights = jnp.exp(jax.random.uniform(jax.random.fold_in(own, position), (blocks,), jnp.float32, smallest / len(shards), largest / len(shards)))
        factor_of = factor_of * jnp.repeat(heights, extent[position] // blocks).reshape([-1 if axis == position else 1 for axis in range(len(extent))])
    return factor_of


def centred(own_key, extent, width, most, cuts=(), kind=jnp.bfloat16):
    array = jax.random.normal(own_key, extent, jnp.float32) * width
    if len(cuts) > 0:
        array = level_of(own_key, extent, cuts, -0.22, 0.18) * array
    return jnp.clip(array, min=-most, max=most).astype(kind)


def setup_inputs(seed: int = 0) -> dict:
    splits = jax.random.split(jax.random.key(seed), 9)
    behaviors = draw_behaviors(jax.random.fold_in(splits[8], 71), 0)
    candidates = draw_candidates(jax.random.fold_in(splits[8], 71), 0)
    lengths = with_ends(jax.random.randint(splits[2], (USERS,), L // 8, L + 1), jax.random.fold_in(splits[2], 1), L // 8, L).astype(jnp.int32)
    bilinear = draw_bilinear(jax.random.fold_in(splits[8], 71), 0)
    norm_gain = jnp.clip(1.0 + 0.18 * jax.random.normal(splits[4], (D,), jnp.float32), 0.1, 1.9)
    w_gate = centred(splits[5], (D, FF), D ** -0.5, 0.125, ((0, 4), (1, 8)))
    w_up = centred(splits[6], (D, FF), D ** -0.5, 0.125, ((0, 4), (1, 8)))
    w_down = centred(splits[7], (FF, D), FF ** -0.5, 0.0625, ((0, 8), (1, 4)))
    return dict(behaviors=behaviors, candidates=candidates, lengths=lengths, bilinear=bilinear, norm_gain=norm_gain, w_gate=w_gate, w_up=w_up, w_down=w_down)


def one_user(items):
    query, behavior, length = items
    scores = jnp.dot(query.T, behavior, preferred_element_type=jnp.float32) * (1.0 / math.sqrt(D))
    live = lax.broadcasted_iota(jnp.int32, (1, L), 1) < length
    masked = jnp.where(live, scores, -1e+30)
    highest = lax.optimization_barrier(jnp.max(masked, axis=-1, keepdims=True))
    expons = jnp.where(live, jnp.exp(masked - highest), 0.0)
    probs = (expons / lax.optimization_barrier(jnp.sum(expons, axis=-1, keepdims=True))).astype(jnp.bfloat16)
    return jnp.dot(behavior, probs.T, preferred_element_type=jnp.float32).astype(jnp.bfloat16)

def reference(behaviors, candidates, lengths, bilinear, norm_gain, w_gate, w_up, w_down):
    query = jnp.einsum('ek,ukc->uec', bilinear.astype(jnp.float32), candidates.astype(jnp.float32), precision=lax.Precision.HIGHEST)
    query = query.astype(jnp.bfloat16)
    pooled = lax.map(one_user, (query, behaviors, lengths))
    values = pooled.astype(jnp.float32)
    square_mean = lax.optimization_barrier(jnp.mean(values * values, axis=1, keepdims=True))
    normed = (values * lax.rsqrt(square_mean + 1e-06) * norm_gain[None, :, None]).astype(jnp.bfloat16)
    flat = jnp.transpose(normed, (0, 2, 1)).reshape(-1, D)
    gate = jnp.dot(flat, w_gate, preferred_element_type=jnp.float32)
    upward = jnp.dot(flat, w_up, preferred_element_type=jnp.float32)
    hidden = (jax.nn.silu(gate) * upward).astype(jnp.bfloat16)
    group_width = FF // N_MP
    hidden_groups = jnp.transpose(hidden.reshape(hidden.shape[0], N_MP, group_width), (1, 0, 2))
    down_groups = w_down.reshape(N_MP, group_width, D)

    def add_group(total, items):
        hidden_part, down_part = items
        part = jnp.dot(hidden_part, down_part, preferred_element_type=jnp.float32).astype(jnp.bfloat16)
        return (total + part.astype(jnp.float32), None)
    start_total = jnp.zeros((hidden.shape[0], D), jnp.float32)
    total, _ = lax.scan(add_group, start_total, (hidden_groups, down_groups))
    interest = total.astype(jnp.bfloat16)
    return jnp.transpose(interest.reshape(USERS, C, D), (0, 2, 1))
```

```python
import math

import jax
import jax.numpy as jnp
from jax import lax
from jax.sharding import PartitionSpec as P


def pick(x, index, size, axis):
    return lax.dynamic_slice_in_dim(x, index * size, size, axis)


def place(whole, part, index, axis):
    return lax.dynamic_update_slice_in_dim(whole, part, index * part.shape[axis], axis)


def swap(x, axis_name, count, offset):
    return lax.ppermute(x, axis_name, [(i, i ^ offset) for i in range(count)])


def attention_weights(scores, live):
    masked = jnp.where(live, scores, -1e30)
    highest = jnp.max(masked, axis=-1, keepdims=True)
    expons = jnp.where(live, jnp.exp(masked - highest), 0.0)
    return (expons / jnp.sum(expons, axis=-1, keepdims=True)).astype(jnp.bfloat16)


def make_shards(dp_count, mp_count):
    chips = mp_count // 2

    def shards(behaviors, candidates, lengths, bilinear, norm_gain, w_gate, w_up, w_down):
        users, width, cands = candidates.shape
        features = bilinear.shape[1]
        length = behaviors.shape[2]
        half = users // 2
        member = lax.axis_index("mp")
        layer = lax.axis_index("dp")
        core, chip = member % 2, member // 2
        parity = layer % 2

        own_cands = pick(candidates, core, half, 0)
        other_cands = pick(candidates, 1 - core, half, 0)
        cand_parts = [own_cands] + [
            swap(own_cands if s % 2 == 0 else other_cands, "mp", mp_count, s)
            for s in range(1, mp_count)
        ]

        def spread(w, axis):
            size = w.shape[axis] // 2
            own, other = pick(w, parity, size, axis), pick(w, 1 - parity, size, axis)
            return [own] + [
                swap(own if s % 2 == 0 else other, "dp", dp_count, s) for s in range(1, dp_count)
            ]

        def join(parts, axis):
            shape = list(parts[0].shape)
            shape[axis] *= dp_count
            whole = jnp.zeros(shape, parts[0].dtype)
            for s, part in enumerate(parts):
                whole = place(whole, part, layer ^ s, axis)
            return whole

        gate_own = join(spread(w_gate, 1), 0)
        up_own = join(spread(w_up, 1), 0)
        down_own = join(spread(w_down, 0), 1)
        gate_w = jnp.concatenate([gate_own, swap(gate_own, "mp", mp_count, 1)], axis=1)
        up_w = jnp.concatenate([up_own, swap(up_own, "mp", mp_count, 1)], axis=1)
        down_w = jnp.concatenate([down_own, swap(down_own, "mp", mp_count, 1)], axis=0)

        chip_behaviors = jnp.concatenate(
            [
                pick(behaviors, core, half, 0),
                swap(pick(behaviors, 1 - core, half, 0), "mp", mp_count, 1),
            ],
            axis=1,
        )
        chip_bilinear = jnp.concatenate(
            [bilinear, swap(bilinear, "mp", mp_count, 1)], axis=0
        )

        all_cands = jnp.zeros((half, features, cands), candidates.dtype)
        for s, part in enumerate(cand_parts):
            all_cands = place(all_cands, part, member ^ s, 1)
        query = jnp.einsum(
            "ek,ukc->uec", chip_bilinear, all_cands, preferred_element_type=jnp.float32
        ).astype(jnp.bfloat16)
        partial = jnp.einsum(
            "ukc,ukl->ucl", query, chip_behaviors, preferred_element_type=jnp.float32
        ).reshape(half * cands, length)
        rows = half * cands // chips
        share = pick(partial, chip, rows, 0)
        for t in range(1, chips):
            share = share + swap(pick(partial, chip ^ t, rows, 0), "mp", mp_count, 2 * t)
        row_lengths = lax.dynamic_slice_in_dim(
            jnp.repeat(lengths, cands), core * half * cands + chip * rows, rows
        )
        live = lax.broadcasted_iota(jnp.int32, (rows, length), 1) < row_lengths[:, None]
        own_probs = attention_weights(share * (1.0 / math.sqrt(features)), live)
        probs = jnp.zeros((half * cands, length), jnp.bfloat16)
        probs = place(probs, own_probs, chip, 0)
        for t in range(1, chips):
            probs = place(probs, swap(own_probs, "mp", mp_count, 2 * t), chip ^ t, 0)
        pooled = jnp.einsum(
            "ucl,ukl->ukc",
            probs.reshape(half, cands, length),
            chip_behaviors,
            preferred_element_type=jnp.float32,
        ).astype(jnp.bfloat16)
        pooled = jnp.where(core == 0, pooled, jnp.roll(pooled, width, axis=1))

        def gather_features(own):
            whole = jnp.zeros((half, features, cands), own.dtype)
            whole = place(whole, own, chip, 1)
            for t in range(1, chips):
                whole = place(whole, swap(own, "mp", mp_count, 2 * t), chip ^ t, 1)
            return whole

        def normed_of(whole):
            values = whole.astype(jnp.float32)
            square_mean = jnp.mean(values * values, axis=1, keepdims=True)
            return (values * lax.rsqrt(square_mean + 1e-06) * norm_gain[None, :, None]).astype(
                jnp.bfloat16
            )

        def feed_forward(whole):
            normed = normed_of(whole)
            gate = jnp.einsum("ukc,kf->ucf", normed, gate_w, preferred_element_type=jnp.float32)
            upward = jnp.einsum("ukc,kf->ucf", normed, up_w, preferred_element_type=jnp.float32)
            hidden = (jax.nn.silu(gate) * upward).astype(jnp.bfloat16)
            return jnp.einsum(
                "ucf,fk->ukc", hidden, down_w, preferred_element_type=jnp.float32
            ).astype(jnp.bfloat16)

        def scatter_features(result):
            total = pick(result, chip, 2 * width, 1).astype(jnp.float32)
            for t in range(1, chips):
                part = swap(pick(result, chip ^ t, 2 * width, 1), "mp", mp_count, 2 * t)
                total = total + part.astype(jnp.float32)
            return total

        partner_pooled = swap(pooled, "dp", dp_count, 1)
        own_whole = gather_features(pooled)
        partner_whole = gather_features(partner_pooled)
        own_result = feed_forward(own_whole)
        partner_result = feed_forward(partner_whole)
        partner_total = scatter_features(partner_result).astype(jnp.bfloat16)
        own_total = scatter_features(own_result)
        interest = (own_total + swap(partner_total, "dp", dp_count, 1).astype(jnp.float32)).astype(
            jnp.bfloat16
        )
        kept = pick(interest, core, width, 1)
        given = swap(pick(interest, 1 - core, width, 1), "mp", mp_count, 1)
        out = jnp.zeros((users, width, cands), jnp.bfloat16)
        out = place(out, kept, core, 0)
        return place(out, given, 1 - core, 0)

    return shards


def solution(mesh):
    return jax.shard_map(
        make_shards(mesh.shape["dp"], mesh.shape["mp"]),
        mesh=mesh,
        in_specs=(
            P("dp", "mp", None),
            P("dp", "mp", None),
            P("dp"),
            P("mp", None),
            P(),
            P("dp", "mp"),
            P("dp", "mp"),
            P("mp", "dp"),
        ),
        out_specs=P("dp", "mp", None),
        check_vma=False,
    )
```

```python
import math

import jax
import jax.numpy as jnp
from jax import lax
from jax.experimental import pallas as pl
from jax.experimental.pallas import tpu as pltpu
from jax.sharding import PartitionSpec as P


VMEM_WHOLE = pl.BlockSpec(memory_space=pltpu.VMEM)
SMEM_WHOLE = pl.BlockSpec(memory_space=pltpu.SMEM)
IN_PLACE = pl.BlockSpec(memory_space=pl.ANY)


def pick(x, index, size, axis):
    return lax.dynamic_slice_in_dim(x, index * size, size, axis)


def swap(x, axis_name, count, offset):
    return lax.ppermute(x, axis_name, [(i, i ^ offset) for i in range(count)])


def dot(a, b, dims):
    return lax.dot_general(a, b, (dims, ((), ())), preferred_element_type=jnp.float32)


def score_parts(where, cand_parts, bilinears, behaviors, rows):
    chips = len(cand_parts)
    half, chip_width, cands = cand_parts[0].shape
    width, features = bilinears[0].shape
    length = behaviors[0].shape[2]
    blocks = cands // rows

    def body(where_ref, *refs):
        cand_refs = refs[:chips]
        bilinear_refs = refs[chips : chips + 2]
        behavior_refs = refs[chips + 2 : chips + 4]
        out_refs = refs[chips + 4 :]
        chip = where_ref[0]
        step = pl.program_id(0)
        queries = []
        for bilinear_ref in bilinear_refs:
            total = jnp.zeros((width, 2 * cands), jnp.float32)
            for t in range(chips):
                start = pl.multiple_of((chip ^ t) * chip_width, chip_width)
                pair = jnp.concatenate([cand_refs[t][0], cand_refs[t][1]], axis=1)
                total += dot(bilinear_ref[:, pl.ds(start, chip_width)], pair, ((1,), (0,)))
            queries.append(total.astype(jnp.bfloat16))
        for i in range(2):
            scores = jnp.zeros((cands, length), jnp.float32)
            for query, behavior_ref in zip(queries, behavior_refs):
                mine = query[:, i * cands : (i + 1) * cands]
                scores += dot(mine, behavior_ref[i], ((0,), (0,)))
            for b in range(blocks):
                target = chip ^ ((2 * step + i) * blocks + b)
                for t in range(chips):

                    @pl.when(target == t)
                    def _():
                        out_refs[t][...] = scores[b * rows : (b + 1) * rows]

    pair_block = lambda shape: pl.BlockSpec((2,) + shape, lambda i: (i, 0, 0))
    whole_block = lambda shape: pl.BlockSpec(shape, lambda i: (0, 0))
    return pl.pallas_call(
        body,
        grid=(half // 2,),
        in_specs=[SMEM_WHOLE]
        + [pair_block((chip_width, cands))] * chips
        + [whole_block((width, features))] * 2
        + [pair_block((width, length))] * 2,
        out_specs=[whole_block((rows, length))] * chips,
        out_shape=[jax.ShapeDtypeStruct((rows, length), jnp.float32)] * chips,
        name="scores",
    )(where, *cand_parts, *bilinears, *behaviors)


def softmax_rows(where, lengths, parts, cands, features):
    rows, length = parts[0].shape
    half = lengths.shape[0] // 2

    def body(where_ref, lengths_ref, *refs):
        part_refs, out_ref = refs[:-1], refs[-1]
        user = where_ref[1] * half + where_ref[0] * rows // cands
        total = part_refs[0][...]
        for part_ref in part_refs[1:]:
            total += part_ref[...]
        scores = total * (1.0 / math.sqrt(features))
        live = lax.broadcasted_iota(jnp.int32, (rows, length), 1) < lengths_ref[user]
        masked = jnp.where(live, scores, -1e30)
        highest = jnp.max(masked, axis=-1, keepdims=True)
        expons = jnp.where(live, jnp.exp(masked - highest), 0.0)
        out_ref[...] = (expons / jnp.sum(expons, axis=-1, keepdims=True)).astype(jnp.bfloat16)

    return pl.pallas_call(
        body,
        in_specs=[SMEM_WHOLE, SMEM_WHOLE] + [VMEM_WHOLE] * len(parts),
        out_specs=VMEM_WHOLE,
        out_shape=jax.ShapeDtypeStruct((rows, length), jnp.bfloat16),
        name="softmax",
    )(where, lengths, *parts)


def pool(where, prob_parts, behaviors, cands):
    chips = len(prob_parts)
    rows, length = prob_parts[0].shape
    half, width, _ = behaviors[0].shape

    def body(where_ref, *refs):
        prob_refs = refs[:chips]
        own_ref, other_ref, out_ref, probs = refs[chips:]
        chip, core = where_ref[0], where_ref[1]
        step = pl.program_id(0)

        @pl.when(step == 0)
        def _():
            for t in range(chips):
                start = pl.multiple_of((chip ^ t) * rows, rows)
                probs[pl.ds(start, rows), :] = prob_refs[t][...]

        mine = probs[pl.ds(pl.multiple_of(step * cands, cands), cands), :]
        for side, ref in ((core, own_ref), (1 - core, other_ref)):
            start = pl.multiple_of(side * width, width)
            out_ref[0, pl.ds(start, width), :] = dot(ref[0], mine, ((1,), (1,))).astype(
                jnp.bfloat16
            )

    user_block = lambda shape: pl.BlockSpec((1,) + shape, lambda i: (i, 0, 0))
    return pl.pallas_call(
        body,
        grid=(half,),
        in_specs=[SMEM_WHOLE]
        + [pl.BlockSpec((rows, length), lambda i: (0, 0))] * chips
        + [user_block((width, length))] * 2,
        out_specs=user_block((2 * width, cands)),
        out_shape=jax.ShapeDtypeStruct((half, 2 * width, cands), jnp.bfloat16),
        scratch_shapes=[pltpu.VMEM((half * cands, length), jnp.bfloat16)],
        name="pool",
    )(where, *prob_parts, *behaviors)


def hidden_units(where, parts, gain, weights):
    chips = len(parts)
    half, chip_width, cands = parts[0].shape
    features = gain.shape[0]
    layers = len(weights[0])
    units, block = weights[0][0].shape
    units //= 2
    lanes = half * cands

    def body(where_ref, *refs):
        part_refs = refs[:chips]
        gain_ref = refs[chips]
        weight_refs = [
            refs[chips + 1 + i * layers : chips + 1 + (i + 1) * layers] for i in range(2)
        ]
        out_ref, raw, normed, packed, sems = refs[chips + 1 + 2 * layers :]
        chip, layer = where_ref[0], where_ref[2]
        copies = []
        for t in range(chips):
            start = pl.multiple_of((chip ^ t) * chip_width, chip_width)
            copies.append(
                pltpu.make_async_copy(
                    part_refs[t], raw.at[:, pl.ds(start, chip_width), :], sems.at[t]
                )
            )
        loads = []
        for i in range(2):
            for s in range(layers):
                start = pl.multiple_of((layer ^ s) * block, block)
                loads.append(
                    pltpu.make_async_copy(
                        weight_refs[i][s],
                        packed.at[i, :, pl.ds(start, block)],
                        sems.at[chips + i * layers + s],
                    )
                )
        for copy in copies + loads:
            copy.start()
        for copy in copies:
            copy.wait()
        for u in range(half):
            chunk = 256 if features % 256 == 0 else features

            def square(k, total):
                rows = pl.ds(pl.multiple_of(k * chunk, chunk), chunk)
                values = raw[u, rows, :].astype(jnp.float32)
                return total + jnp.sum(values * values, axis=0, keepdims=True)

            total = lax.fori_loop(
                0, features // chunk, square, jnp.zeros((1, cands), jnp.float32)
            )
            scale = lax.rsqrt(total * (1.0 / features) + 1e-06)

            def apply(k, carry):
                rows = pl.ds(pl.multiple_of(k * chunk, chunk), chunk)
                values = raw[u, rows, :].astype(jnp.float32)
                normed[rows, u * cands : (u + 1) * cands] = (
                    values * scale * gain_ref[rows, :]
                ).astype(jnp.bfloat16)
                return carry

            lax.fori_loop(0, features // chunk, apply, 0)
        for i in range(2):
            for s in range(layers):
                loads[i * layers + s].wait()
            tile = min(256, units)
            for f in range(0, units, tile):
                gate = dot(packed[i, f : f + tile, :], normed[...], ((1,), (0,)))
                upward = dot(
                    packed[i, units + f : units + f + tile, :], normed[...], ((1,), (0,))
                )
                out_ref[i * units + f : i * units + f + tile, :] = (
                    gate / (1.0 + jnp.exp(-gate)) * upward
                ).astype(jnp.bfloat16)

    return pl.pallas_call(
        body,
        in_specs=[SMEM_WHOLE] + [IN_PLACE] * chips + [VMEM_WHOLE] + [IN_PLACE] * (2 * layers),
        out_specs=VMEM_WHOLE,
        out_shape=jax.ShapeDtypeStruct((2 * units, lanes), jnp.bfloat16),
        scratch_shapes=[
            pltpu.VMEM((half, features, cands), jnp.bfloat16),
            pltpu.VMEM((features, lanes), jnp.bfloat16),
            pltpu.VMEM((2, 2 * units, features), jnp.bfloat16),
            pltpu.SemaphoreType.DMA((chips + 2 * layers,)),
        ],
        name="hidden",
    )(where, *parts, gain, *weights[0], *weights[1])


def down_parts(where, hidden, weights, chips, cands):
    layers = len(weights[0])
    block, units = weights[0][0].shape
    features = block * layers
    chip_width = features // chips
    lanes = hidden.shape[1]
    half = lanes // cands

    def body(where_ref, hidden_ref, *refs):
        weight_refs = [refs[i * layers : (i + 1) * layers] for i in range(2)]
        out_refs = refs[2 * layers : 2 * layers + chips]
        packed, sems = refs[2 * layers + chips :]
        chip, layer = where_ref[0], where_ref[2]
        loads = []
        for i in range(2):
            for s in range(layers):
                start = pl.multiple_of((layer ^ s) * block, block)
                loads.append(
                    pltpu.make_async_copy(
                        weight_refs[i][s],
                        packed.at[pl.ds(start, block), pl.ds(i * units, units)],
                        sems.at[i * layers + s],
                    )
                )
        for load in loads:
            load.start()
        for load in loads:
            load.wait()
        for t in range(chips - 1, -1, -1):
            start = pl.multiple_of((chip ^ t) * chip_width, chip_width)
            result = dot(
                packed[pl.ds(start, chip_width), :], hidden_ref[...], ((1,), (0,))
            ).astype(jnp.bfloat16)
            for u in range(half):
                out_refs[t][u] = result[:, u * cands : (u + 1) * cands]

    return pl.pallas_call(
        body,
        in_specs=[SMEM_WHOLE, VMEM_WHOLE] + [IN_PLACE] * (2 * layers),
        out_specs=[VMEM_WHOLE] * chips,
        out_shape=[jax.ShapeDtypeStruct((half, chip_width, cands), jnp.bfloat16)] * chips,
        scratch_shapes=[
            pltpu.VMEM((features, 2 * units), jnp.bfloat16),
            pltpu.SemaphoreType.DMA((2 * layers,)),
        ],
        name="down",
    )(where, hidden, *weights[0], *weights[1])


def make_shards(dp_count, mp_count):
    chips = mp_count // 2

    def across(x, t):
        return swap(x, "mp", mp_count, 2 * t)

    def beside(x):
        return swap(x, "mp", mp_count, 1)

    def to_chips(x):
        return [x] + [across(x, t) for t in range(chips - 1, 0, -1)][::-1]

    def shards(behaviors, candidates, lengths, bilinear, norm_gain, w_gate, w_up, w_down):
        users, width, cands = candidates.shape
        features = bilinear.shape[1]
        half = users // 2
        rows = half * cands // chips
        member, layer = lax.axis_index("mp"), lax.axis_index("dp")
        core, chip = member % 2, member // 2
        parity = layer % 2
        where = jnp.stack([chip, core, layer]).astype(jnp.int32)

        own_cands = pick(candidates, core, half, 0)
        given_cands = beside(pick(candidates, 1 - core, half, 0))
        first = jnp.where(core == 0, own_cands, given_cands)
        second = jnp.where(core == 0, given_cands, own_cands)
        cand_parts = to_chips(jnp.concatenate([first, second], axis=1))

        units = w_down.shape[0] // 2

        def spread(own, other):
            order = [s for s in range(2, dp_count)] + [1]
            got = {0: own}
            for s in order:
                got[s] = swap(own if s % 2 == 0 else other, "dp", dp_count, s)
            return [got[s] for s in range(dp_count)]

        gate_t, up_t, down_t = w_gate.T, w_up.T, w_down.T

        def gate_up(which):
            return jnp.concatenate([pick(gate_t, which, units, 0), pick(up_t, which, units, 0)])

        expand_own = spread(gate_up(parity), gate_up(1 - parity))
        down_own = spread(pick(down_t, parity, units, 1), pick(down_t, 1 - parity, units, 1))

        bilinears = [bilinear, beside(bilinear)]
        behavior_sides = [
            pick(behaviors, core, half, 0),
            beside(pick(behaviors, 1 - core, half, 0)),
        ]
        gain = jnp.broadcast_to(norm_gain[:, None], (features, cands))

        shares = score_parts(where, cand_parts, bilinears, behavior_sides, rows)
        parts = [shares[0]] + [across(shares[t], t) for t in range(chips - 1, 0, -1)]
        probs = softmax_rows(where, lengths, parts, cands, features)
        prob_parts = to_chips(probs)
        pooled = pool(where, prob_parts, behavior_sides, cands)

        partner_pooled = swap(pooled, "dp", dp_count, 1)
        own_parts = to_chips(pooled)
        pooled, expand_own = lax.optimization_barrier((pooled, expand_own))
        expand = [expand_own, [beside(w) for w in expand_own]]
        partner_parts = to_chips(partner_pooled)
        own_hidden = hidden_units(where, own_parts, gain, expand)
        own_hidden, down_own = lax.optimization_barrier((own_hidden, down_own))
        down = [down_own, [beside(w) for w in down_own]]
        partner_hidden = hidden_units(where, partner_parts, gain, expand)

        def scatter(results):
            total = results[0].astype(jnp.float32)
            for t in range(chips - 1, 0, -1):
                total = total + across(results[t], t).astype(jnp.float32)
            return total

        partner_total = scatter(down_parts(where, partner_hidden, down, chips, cands))
        returned = swap(partner_total.astype(jnp.bfloat16), "dp", dp_count, 1)
        own_total = scatter(down_parts(where, own_hidden, down, chips, cands))
        interest = (own_total + returned.astype(jnp.float32)).astype(jnp.bfloat16)
        kept = pick(interest, core, width, 1)
        given = beside(pick(interest, 1 - core, width, 1))
        return jnp.concatenate(
            [jnp.where(core == 0, kept, given), jnp.where(core == 0, given, kept)], axis=0
        )

    return shards


def solution(mesh):
    return jax.shard_map(
        make_shards(mesh.shape["dp"], mesh.shape["mp"]),
        mesh=mesh,
        in_specs=(
            P("dp", "mp", None),
            P("dp", "mp", None),
            P("dp"),
            P("mp", None),
            P(),
            P("dp", "mp"),
            P("dp", "mp"),
            P("mp", "dp"),
        ),
        out_specs=P("dp", "mp", None),
        check_vma=False,
    )
```

```python
import math

import jax
import jax.numpy as jnp
from jax import lax
from jax.experimental import pallas as pl
from jax.experimental.pallas import tpu as pltpu
from jax.sharding import PartitionSpec as P


VMEM_WHOLE = pl.BlockSpec(memory_space=pltpu.VMEM)
SMEM_WHOLE = pl.BlockSpec(memory_space=pltpu.SMEM)
IN_PLACE = pl.BlockSpec(memory_space=pltpu.HBM)


def pick(x, index, size, axis):
    return lax.dynamic_slice_in_dim(x, index * size, size, axis)


def swap(x, axis_name, count, offset):
    return lax.ppermute(x, axis_name, [(i, i ^ offset) for i in range(count)])


def dot(a, b, dims):
    return lax.dot_general(a, b, (dims, ((), ())), preferred_element_type=jnp.float32)


def score_parts(where, cand_parts, bilinears, behaviors, rows, which):
    chips = len(cand_parts)
    group, chip_width, cands = cand_parts[0].shape
    width, features = bilinears[0].shape
    users, _, length = behaviors[0].shape
    blocks = cands // rows
    steps = group // 2

    def body(where_ref, *refs):
        cand_refs = refs[:chips]
        bilinear_refs = refs[chips : chips + 2]
        behavior_refs = refs[chips + 2 : chips + 4]
        out_refs = refs[chips + 4 :]
        chip, core = where_ref[0], where_ref[1]
        step = pl.program_id(0)
        queries = []
        for bilinear_ref in bilinear_refs:
            total = jnp.zeros((width, 2 * cands), jnp.float32)
            for t in range(chips):
                pair = jnp.concatenate([cand_refs[t][0], cand_refs[t][1]], axis=1)
                start = pl.multiple_of((chip ^ t) * chip_width, chip_width)
                if width % 128:
                    swapped = jnp.concatenate([pair[width:], pair[:width]], axis=0)
                    pair = jnp.where(core == 0, pair, swapped)
                    total += dot(bilinear_ref[:, pl.ds(start, chip_width)], pair, ((1,), (0,)))
                    continue
                for side in range(2):
                    at = pl.ds(pl.multiple_of(start + (core ^ side) * width, width), width)
                    part = pair[side * width : (side + 1) * width]
                    total += dot(bilinear_ref[:, at], part, ((1,), (0,)))
            queries.append(total.astype(jnp.bfloat16))
        for i in range(2):
            scores = jnp.zeros((cands, length), jnp.float32)
            for query, behavior_ref in zip(queries, behavior_refs):
                mine = query[:, i * cands : (i + 1) * cands]
                scores += dot(mine, behavior_ref[i], ((0,), (0,)))
            for b in range(blocks):
                target = chip ^ ((2 * step + i) * blocks + b)
                for t in range(chips):

                    @pl.when(target == t)
                    def _():
                        out_refs[t][...] = scores[b * rows : (b + 1) * rows]

    pair_block = lambda shape: pl.BlockSpec((2,) + shape, lambda i, w: (i, 0, 0))
    mine_block = lambda shape: pl.BlockSpec((2,) + shape, lambda i, w: ((w[1] * (users // 2) + which * group) // 2 + i, 0, 0))
    whole_block = lambda shape: pl.BlockSpec(shape, lambda i, w: (0, 0))
    return pl.pallas_call(
        body,
        grid_spec=pltpu.PrefetchScalarGridSpec(
            num_scalar_prefetch=1,
            grid=(steps,),
            in_specs=[pair_block((chip_width, cands))] * chips
            + [whole_block((width, features))] * 2
            + [mine_block((width, length))] * 2,
            out_specs=[whole_block((rows, length))] * chips,
        ),
        out_shape=[jax.ShapeDtypeStruct((rows, length), jnp.float32)] * chips,
        name="scores",
    )(where, *cand_parts, *bilinears, *behaviors)


def softmax_rows(where, lengths, parts, cands, features, which):
    rows, length = parts[0].shape
    half = lengths.shape[0] // 2

    def body(where_ref, lengths_ref, *refs):
        part_refs, out_ref = refs[:-1], refs[-1]
        user = where_ref[1] * half + which * (half // 2) + where_ref[0] * rows // cands
        total = part_refs[0][...]
        for part_ref in part_refs[1:]:
            total += part_ref[...]
        scores = total * (1.0 / math.sqrt(features))
        live = lax.broadcasted_iota(jnp.int32, (rows, length), 1) < lengths_ref[user]
        masked = jnp.where(live, scores, -1e30)
        highest = jnp.max(masked, axis=-1, keepdims=True)
        expons = jnp.where(live, jnp.exp(masked - highest), 0.0)
        out_ref[...] = (expons / jnp.sum(expons, axis=-1, keepdims=True)).astype(jnp.bfloat16)

    return pl.pallas_call(
        body,
        in_specs=[SMEM_WHOLE, SMEM_WHOLE] + [VMEM_WHOLE] * len(parts),
        out_specs=VMEM_WHOLE,
        out_shape=jax.ShapeDtypeStruct((rows, length), jnp.bfloat16),
        name="softmax",
    )(where, lengths, *parts)


def pool(where, prob_parts, behaviors, cands, which):
    chips = len(prob_parts)
    rows, length = prob_parts[0].shape
    users, width, _ = behaviors[0].shape
    half = users // 2
    group = half // 2

    def body(where_ref, *refs):
        prob_refs = refs[:chips]
        own_ref, other_ref, out_ref, probs = refs[chips:]
        chip, core = where_ref[0], where_ref[1]
        step = pl.program_id(0)

        @pl.when(step == 0)
        def _():
            for t in range(chips):
                start = pl.multiple_of((chip ^ t) * rows, rows)
                probs[pl.ds(start, rows), :] = prob_refs[t][...]

        mine = probs[pl.ds(pl.multiple_of(step * cands, cands), cands), :]
        for side, ref in ((core, own_ref), (1 - core, other_ref)):
            start = pl.multiple_of(side * width, width)
            out_ref[0, pl.ds(start, width), :] = dot(ref[0], mine, ((1,), (1,))).astype(
                jnp.bfloat16
            )

    mine_block = pl.BlockSpec(
        (1, width, length), lambda i, w: (w[1] * half + which * group + i, 0, 0)
    )
    return pl.pallas_call(
        body,
        grid_spec=pltpu.PrefetchScalarGridSpec(
            num_scalar_prefetch=1,
            grid=(group,),
            in_specs=[pl.BlockSpec((rows, length), lambda i, w: (0, 0))] * chips
            + [mine_block] * 2,
            out_specs=pl.BlockSpec((1, 2 * width, cands), lambda i, w: (i, 0, 0)),
            scratch_shapes=[pltpu.VMEM((group * cands, length), jnp.bfloat16)],
        ),
        out_shape=jax.ShapeDtypeStruct((group, 2 * width, cands), jnp.bfloat16),
        name="pool",
    )(where, *prob_parts, *behaviors)


def pack_weights(where, arrays, axis, row=None, lanes=0):
    units = arrays[0].shape[axis] // 2
    depth = arrays[0].shape[1 - axis]
    count = len(arrays)

    def body(where_ref, *refs):
        for which in range(2):
            start = pl.multiple_of((where_ref[3] ^ which) * units, units)
            for i in range(count):
                if axis == 1:
                    value = refs[i][:, pl.ds(start, units)]
                    refs[count + which][i * units : (i + 1) * units, :] = value.T
                else:
                    refs[extra + which][...] = refs[i][pl.ds(start, units), :].T
        if row is not None:
            refs[-1][...] = jnp.broadcast_to(refs[count][...], (lanes, row.shape[1])).T

    shape = (count * units, depth) if axis == 1 else (depth, units)
    out_shape = [jax.ShapeDtypeStruct(shape, jnp.bfloat16)] * 2
    if row is not None:
        arrays = (*arrays, row)
        out_shape += [jax.ShapeDtypeStruct((row.shape[1], lanes), row.dtype)]
    extra = len(arrays)
    return pl.pallas_call(
        body,
        in_specs=[SMEM_WHOLE] + [VMEM_WHOLE] * extra,
        out_specs=[VMEM_WHOLE] * len(out_shape),
        out_shape=out_shape,
        name="pack",
    )(where, *arrays)


def start_loads(sems, base, pairs):
    copies = []
    for i, (source, target) in enumerate(pairs):
        copies.append(pltpu.make_async_copy(source, target, sems.at[base + i]))
        copies[-1].start()
    return copies


def normalize(raw, normed, gain_ref):
    users, features, cands = raw.shape
    chunk = 256 if features % 256 == 0 else features
    for u in range(users):

        def square(k, total):
            rows = pl.ds(pl.multiple_of(k * chunk, chunk), chunk)
            values = raw[u, rows, :].astype(jnp.float32)
            return total + jnp.sum(values * values, axis=0, keepdims=True)

        total = lax.fori_loop(0, features // chunk, square, jnp.zeros((1, cands), jnp.float32))
        scale = lax.rsqrt(total * (1.0 / features) + 1e-06)

        def apply(k, carry):
            rows = pl.ds(pl.multiple_of(k * chunk, chunk), chunk)
            values = raw[u, rows, :].astype(jnp.float32)
            normed[rows, u * cands : (u + 1) * cands] = (
                values * scale * gain_ref[rows, :]
            ).astype(jnp.bfloat16)
            return carry

        lax.fori_loop(0, features // chunk, apply, 0)


def feed_forward(where, groups, orders, gain, expand, down, hidden=None):
    count, chips = len(groups), len(groups[0])
    size, chip_width, cands = groups[0][0].shape
    features = gain.shape[0]
    weights = expand if hidden is None else down
    layers = len(weights[0])
    units = expand[0][0].shape[0] // 2
    block = features // layers
    lanes = size * cands
    expands, downs = hidden is None, down is not None
    outs = chips if orders is None else 2

    def body(where_ref, *refs):
        refs = list(refs)
        take = lambda n: [refs.pop(0) for _ in range(n)]
        chip, layer = where_ref[0], where_ref[2]
        at_chip = lambda t: pl.ds(pl.multiple_of((chip ^ t) * chip_width, chip_width), chip_width)
        at_layer = lambda s: pl.ds(pl.multiple_of((layer ^ s) * block, block), block)
        if expands:
            part_refs = take(count * chips)
            (gain_ref,) = take(1)
            expand_refs = take(2 * layers)
        else:
            (hidden_ref,) = take(1)
        if downs:
            down_refs = take(2 * layers)
            out_refs = take(outs * count)
            if expands:
                (hidden_ref,) = take(1)
        else:
            (hidden_ref,) = take(1)
        (sems,) = take(1)
        if expands:
            raw, normed, wide = take(3)
            part_loads = start_loads(
                sems,
                0,
                [
                    (part_refs[g * chips + t], raw.at[pl.ds(g * size, size), at_chip(t), :])
                    for g in range(count)
                    for t in range(chips)
                ],
            )
            expand_loads = start_loads(
                sems,
                count * chips,
                [
                    (expand_refs[i * layers + s], wide.at[i, :, at_layer(s)])
                    for i in range(2)
                    for s in range(layers)
                ],
            )
        if downs:
            (narrow,) = take(1)
            down_loads = start_loads(
                sems,
                count * chips + 2 * layers,
                [
                    (down_refs[i * layers + s], narrow.at[at_layer(s), pl.ds(i * units, units)])
                    for i in range(2)
                    for s in range(layers)
                ],
            )
        if expands:
            for copy in part_loads:
                copy.wait()
            normalize(raw, normed, gain_ref)
            tile = min(256, units)
            for i in range(2):
                for s in range(layers):
                    expand_loads[i * layers + s].wait()
                for f in range(0, units, tile):
                    gate = dot(wide[i, f : f + tile, :], normed[...], ((1,), (0,)))
                    upward = dot(
                        wide[i, units + f : units + f + tile, :], normed[...], ((1,), (0,))
                    )
                    hidden_ref[i * units + f : i * units + f + tile, :] = (
                        gate / (1.0 + jnp.exp(-gate)) * upward
                    ).astype(jnp.bfloat16)
        if downs:
            for copy in down_loads:
                copy.wait()
            for g in range(count):
                for i in range(chips):
                    target = chips - 1 - i if orders is None else orders[g][i]
                    result = dot(
                        narrow[at_chip(target), :],
                        hidden_ref[:, g * lanes : (g + 1) * lanes],
                        ((1,), (0,)),
                    ).astype(jnp.bfloat16)
                    for u in range(size):
                        mine = result[:, u * cands : (u + 1) * cands]
                        if orders is None:
                            out_refs[chips * g + target][u] = mine
                        else:
                            out_refs[2 * g + (i >= chips // 2)][i % (chips // 2), u] = mine

    total = count * lanes
    hidden_shape = (2 * units, total)
    inputs, in_specs, scratch = [where], [SMEM_WHOLE], []
    if expands:
        inputs += sum(groups, []) + [gain] + expand[0] + expand[1]
        in_specs += [IN_PLACE] * (count * chips) + [VMEM_WHOLE] + [IN_PLACE] * (2 * layers)
        scratch += [
            pltpu.VMEM((count * size, features, cands), jnp.bfloat16),
            pltpu.VMEM((features, total), jnp.bfloat16),
            pltpu.VMEM((2, 2 * units, features), jnp.bfloat16),
        ]
    else:
        inputs += [hidden]
        in_specs += [VMEM_WHOLE]
    scratch = [pltpu.SemaphoreType.DMA((count * chips + 4 * layers,))] + scratch
    if downs:
        inputs += down[0] + down[1]
        in_specs += [IN_PLACE] * (2 * layers)
        shape = (size, chip_width, cands)
        if orders is not None:
            shape = (chips // 2,) + shape
        out_shape = [jax.ShapeDtypeStruct(shape, jnp.bfloat16)] * (outs * count)
        scratch += [pltpu.VMEM((features, 2 * units), jnp.bfloat16)]
        if expands:
            scratch = [pltpu.VMEM(hidden_shape, jnp.bfloat16)] + scratch
    else:
        out_shape = [jax.ShapeDtypeStruct(hidden_shape, jnp.bfloat16)]
    return pl.pallas_call(
        body,
        in_specs=in_specs,
        out_specs=[VMEM_WHOLE] * len(out_shape),
        out_shape=out_shape,
        scratch_shapes=scratch,
        name="feed_forward",
    )(*inputs)


def make_shards(dp_count, mp_count):
    chips = mp_count // 2

    def across(x, t):
        return swap(x, "mp", mp_count, 2 * t)

    def beside(x):
        return swap(x, "mp", mp_count, 1)

    def to_chips(x):
        return [x] + [across(x, t) for t in range(chips - 1, 0, -1)][::-1]

    bits = [1 << i for i in range((chips - 1).bit_length())]

    def doubled(x, order):
        parts = {0: x}
        for bit in order:
            new = {bit: across(x, bit)}
            new.update({t | bit: across(part, bit) for t, part in parts.items() if t})
            parts.update(new)
        return [parts[t] for t in range(chips)]

    def block_order(order):
        blocks = [0]
        for bit in order[::-1]:
            blocks = blocks + [t | bit for t in blocks]
        return blocks

    def halved(near, far, order):
        for bit in order:
            got = across(far, bit)
            total = near.astype(jnp.float32) + got.astype(jnp.float32)
            count = total.shape[0] // 2
            near = total[:count]
            far = total[count:].astype(jnp.bfloat16)
        return total[0]

    def shards(behaviors, candidates, lengths, bilinear, norm_gain, w_gate, w_up, w_down):
        users, width, cands = candidates.shape
        features = bilinear.shape[1]
        half = users // 2
        group = half // 2
        rows = group * cands // chips
        member, layer = lax.axis_index("mp"), lax.axis_index("dp")
        core, chip = member % 2, member // 2
        far_layer = dp_count // 2
        side = layer // far_layer
        where = jnp.stack([chip, core, layer, side]).astype(jnp.int32)

        given_cands = beside(candidates)
        cand_parts = []
        for g in range(2):
            own_cands = jnp.concatenate(
                [pick(x, core * 2 + g, group, 0) for x in (candidates, given_cands)], axis=1
            )
            cand_parts.append(to_chips(own_cands))
        behavior_sides = [behaviors, beside(behaviors)]
        bilinears = [bilinear, beside(bilinear)]

        def layer_swap(x, s):
            return swap(x, "dp", dp_count, s)

        def spread(own, other):
            got = {far_layer: layer_swap(other, far_layer), 0: own}
            for s in range(1, far_layer):
                got[s] = layer_swap(own, s)
            return got

        def forward(got):
            return [
                got[s] if s in got else layer_swap(got[far_layer], s ^ far_layer)
                for s in range(dp_count)
            ]

        expand_got = spread(*pack_weights(where, (w_gate, w_up), 1))
        *down_packs, gain = pack_weights(where, (w_down,), 0, norm_gain[None, :], cands)
        down_got = spread(*down_packs)
        parts, pooled = [], []
        for g in range(2):
            shares = score_parts(where, cand_parts[g], bilinears, behavior_sides, rows, g)
            parts.append([shares[0]] + [across(shares[t], t) for t in range(chips - 1, 0, -1)])
        expand_own = forward(expand_got)
        down_own = forward(down_got)
        for g in range(2):
            probs = softmax_rows(where, lengths, parts[g], cands, features, g)
            prob_parts = to_chips(probs)
            pooled.append(pool(where, prob_parts, behavior_sides, cands, g))
        orders = [bits, bits[::-1]]

        partner_pooled, own_parts, partner_parts = [], [], []
        for g in range(2):
            partner_pooled.append(layer_swap(pooled[g], far_layer))
            own_parts.append(doubled(pooled[g], orders[g]))
            partner_parts.append(to_chips(partner_pooled[g]))

        def besides(pieces):
            other = []
            for piece in pieces:
                other.append(beside(piece))
            return [pieces, other]

        expand = besides(expand_own)
        down = besides(down_own)
        blocks = [block_order(order) for order in orders]
        (own_hidden,) = feed_forward(where, own_parts, blocks, gain, expand, None)
        (partner_hidden,) = feed_forward(where, [partner_parts[0]], None, gain, expand, None)
        totals = []
        for g in range(2):
            shares = feed_forward(
                where, [partner_parts[g]], None, gain, expand, down, (partner_hidden, None)[g]
            )
            total = shares[0].astype(jnp.float32)
            for t in range(chips - 1, 0, -1):
                total = total + across(shares[t], t).astype(jnp.float32)
            totals.append(layer_swap(total.astype(jnp.bfloat16), far_layer))
        own_blocks = feed_forward(where, own_parts, blocks, gain, expand, down, own_hidden)
        interest = []
        for i, order in enumerate(orders):
            interest.append(
                halved(*own_blocks[2 * i : 2 * i + 2], order) + totals[i].astype(jnp.float32)
            )
        interest = jnp.concatenate(interest, axis=0).astype(jnp.bfloat16)
        kept = pick(interest, core, width, 1)
        given = beside(pick(interest, 1 - core, width, 1))
        return jnp.concatenate(
            [jnp.where(core == 0, kept, given), jnp.where(core == 0, given, kept)], axis=0
        )

    return shards


def solution(mesh):
    return jax.shard_map(
        make_shards(mesh.shape["dp"], mesh.shape["mp"]),
        mesh=mesh,
        in_specs=(
            P("dp", "mp", None),
            P("dp", "mp", None),
            P("dp"),
            P("mp", None),
            P(),
            P("dp", "mp"),
            P("dp", "mp"),
            P("mp", "dp"),
        ),
        out_specs=P("dp", "mp", None),
        check_vma=False,
    )
```

```python
import math

import jax
import jax.numpy as jnp
from jax import lax
from jax.experimental import pallas as pl
from jax.experimental.pallas import tpu as pltpu
from jax.sharding import PartitionSpec as P


VMEM_WHOLE = pl.BlockSpec(memory_space=pltpu.VMEM)
SMEM_WHOLE = pl.BlockSpec(memory_space=pltpu.SMEM)
IN_PLACE = pl.BlockSpec(memory_space=pltpu.HBM)


def pick(x, index, size, axis):
    return lax.dynamic_slice_in_dim(x, index * size, size, axis)


def swap(x, axis_name, count, offset):
    return lax.ppermute(x, axis_name, [(i, i ^ offset) for i in range(count)])


def dot(a, b, dims):
    return lax.dot_general(a, b, (dims, ((), ())), preferred_element_type=jnp.float32)


def score_parts(where, cand_parts, bilinears, behaviors, rows, which):
    chips = len(cand_parts)
    group, chip_width, cands = cand_parts[0].shape
    width, features = bilinears[0].shape
    users, _, length = behaviors[0].shape
    blocks = cands // rows
    steps = group // 2

    def body(where_ref, *refs):
        cand_refs = refs[:chips]
        bilinear_refs = refs[chips : chips + 2]
        behavior_refs = refs[chips + 2 : chips + 4]
        out_refs = refs[chips + 4 :]
        chip, core = where_ref[0], where_ref[1]
        step = pl.program_id(0)
        queries = []
        for bilinear_ref in bilinear_refs:
            total = jnp.zeros((width, 2 * cands), jnp.float32)
            for t in range(chips):
                pair = jnp.concatenate([cand_refs[t][0], cand_refs[t][1]], axis=1)
                start = pl.multiple_of((chip ^ t) * chip_width, chip_width)
                if width % 128:
                    swapped = jnp.concatenate([pair[width:], pair[:width]], axis=0)
                    pair = jnp.where(core == 0, pair, swapped)
                    total += dot(bilinear_ref[:, pl.ds(start, chip_width)], pair, ((1,), (0,)))
                    continue
                for side in range(2):
                    at = pl.ds(pl.multiple_of(start + (core ^ side) * width, width), width)
                    part = pair[side * width : (side + 1) * width]
                    total += dot(bilinear_ref[:, at], part, ((1,), (0,)))
            queries.append(total.astype(jnp.bfloat16))
        for i in range(2):
            scores = jnp.zeros((cands, length), jnp.float32)
            for query, behavior_ref in zip(queries, behavior_refs):
                mine = query[:, i * cands : (i + 1) * cands]
                scores += dot(mine, behavior_ref[i], ((0,), (0,)))
            for b in range(blocks):
                target = chip ^ ((2 * step + i) * blocks + b)
                for t in range(chips):

                    @pl.when(target == t)
                    def _():
                        out_refs[t][...] = scores[b * rows : (b + 1) * rows]

    pair_block = lambda shape: pl.BlockSpec((2,) + shape, lambda i, w: (i, 0, 0))
    mine_block = lambda shape: pl.BlockSpec((2,) + shape, lambda i, w: ((w[1] * (users // 2) + which * group) // 2 + i, 0, 0))
    whole_block = lambda shape: pl.BlockSpec(shape, lambda i, w: (0, 0))
    return pl.pallas_call(
        body,
        grid_spec=pltpu.PrefetchScalarGridSpec(
            num_scalar_prefetch=1,
            grid=(steps,),
            in_specs=[pair_block((chip_width, cands))] * chips
            + [whole_block((width, features))] * 2
            + [mine_block((width, length))] * 2,
            out_specs=[whole_block((rows, length))] * chips,
        ),
        out_shape=[jax.ShapeDtypeStruct((rows, length), jnp.float32)] * chips,
        name="scores",
    )(where, *cand_parts, *bilinears, *behaviors)


def softmax_rows(where, lengths, parts, cands, features, which):
    rows, length = parts[0].shape
    half = lengths.shape[0] // 2

    def body(where_ref, lengths_ref, *refs):
        part_refs, out_ref = refs[:-1], refs[-1]
        user = where_ref[1] * half + which * (half // 2) + where_ref[0] * rows // cands
        total = part_refs[0][...]
        for part_ref in part_refs[1:]:
            total += part_ref[...]
        scores = total * (1.0 / math.sqrt(features))
        live = lax.broadcasted_iota(jnp.int32, (rows, length), 1) < lengths_ref[user]
        masked = jnp.where(live, scores, -1e30)
        highest = jnp.max(masked, axis=-1, keepdims=True)
        expons = jnp.where(live, jnp.exp(masked - highest), 0.0)
        out_ref[...] = (expons / jnp.sum(expons, axis=-1, keepdims=True)).astype(jnp.bfloat16)

    return pl.pallas_call(
        body,
        in_specs=[SMEM_WHOLE, SMEM_WHOLE] + [VMEM_WHOLE] * len(parts),
        out_specs=VMEM_WHOLE,
        out_shape=jax.ShapeDtypeStruct((rows, length), jnp.bfloat16),
        name="softmax",
    )(where, lengths, *parts)


def pool(where, prob_parts, behaviors, cands, which):
    chips = len(prob_parts)
    rows, length = prob_parts[0].shape
    users, width, _ = behaviors[0].shape
    half = users // 2
    group = half // 2

    def body(where_ref, *refs):
        prob_refs = refs[:chips]
        own_ref, other_ref, out_ref, probs = refs[chips:]
        chip, core = where_ref[0], where_ref[1]
        step = pl.program_id(0)

        @pl.when(step == 0)
        def _():
            for t in range(chips):
                start = pl.multiple_of((chip ^ t) * rows, rows)
                probs[pl.ds(start, rows), :] = prob_refs[t][...]

        mine = probs[pl.ds(pl.multiple_of(step * cands, cands), cands), :]
        for side, ref in ((core, own_ref), (1 - core, other_ref)):
            start = pl.multiple_of(side * width, width)
            out_ref[0, pl.ds(start, width), :] = dot(ref[0], mine, ((1,), (1,))).astype(
                jnp.bfloat16
            )

    mine_block = pl.BlockSpec(
        (1, width, length), lambda i, w: (w[1] * half + which * group + i, 0, 0)
    )
    return pl.pallas_call(
        body,
        grid_spec=pltpu.PrefetchScalarGridSpec(
            num_scalar_prefetch=1,
            grid=(group,),
            in_specs=[pl.BlockSpec((rows, length), lambda i, w: (0, 0))] * chips
            + [mine_block] * 2,
            out_specs=pl.BlockSpec((1, 2 * width, cands), lambda i, w: (i, 0, 0)),
            scratch_shapes=[pltpu.VMEM((group * cands, length), jnp.bfloat16)],
        ),
        out_shape=jax.ShapeDtypeStruct((group, 2 * width, cands), jnp.bfloat16),
        name="pool",
    )(where, *prob_parts, *behaviors)


def tile_of(units):
    return min(256, units)


def pack_expand(gate, up, far_layer):
    depth, units = gate.shape[0], gate.shape[1] // 2
    tile = tile_of(units)
    tiles = units // tile

    def body(gate_ref, up_ref, own_ref, other_ref, gates, ups, outs, sems):
        side = lax.axis_index("dp") // far_layer
        loads = []
        for k, which in enumerate((1, 0)):
            at = pl.ds(pl.multiple_of((side ^ which) * units, units), units)
            for i, (ref, buffer) in enumerate(((gate_ref, gates), (up_ref, ups))):
                loads.append(pltpu.make_async_copy(ref.at[:, at], buffer.at[k], sems.at[k, i]))
                loads[-1].start()
        stores = []
        for k, target in enumerate((other_ref, own_ref)):
            for i, buffer in enumerate((gates, ups)):
                loads[2 * k + i].wait()
                for f in range(tiles):
                    outs[k, (2 * f + i) * tile : (2 * f + i + 1) * tile, :] = buffer[
                        k, :, f * tile : (f + 1) * tile
                    ].T
            stores.append(pltpu.make_async_copy(outs.at[k], target, sems.at[k, 2]))
            stores[-1].start()
        for store in stores:
            store.wait()

    return pl.pallas_call(
        body,
        in_specs=[IN_PLACE] * 2,
        out_specs=[IN_PLACE] * 2,
        out_shape=[jax.ShapeDtypeStruct((2 * units, depth), gate.dtype)] * 2,
        scratch_shapes=[
            pltpu.VMEM((2, depth, units), gate.dtype),
            pltpu.VMEM((2, depth, units), gate.dtype),
            pltpu.VMEM((2, 2 * units, depth), gate.dtype),
            pltpu.SemaphoreType.DMA((2, 3)),
        ],
        name="pack_expand",
    )(gate, up)


def pack_down(where, down, row, lanes):
    units, width = down.shape[0] // 2, down.shape[1]

    def body(where_ref, down_ref, row_ref, own_ref, other_ref, column_ref):
        for which, ref in enumerate((own_ref, other_ref)):
            start = pl.multiple_of((where_ref[3] ^ which) * units, units)
            ref[...] = down_ref[pl.ds(start, units), :].T
        column_ref[...] = jnp.broadcast_to(row_ref[...], (lanes, row.shape[1])).T

    return pl.pallas_call(
        body,
        in_specs=[SMEM_WHOLE] + [VMEM_WHOLE] * 2,
        out_specs=[VMEM_WHOLE] * 3,
        out_shape=[jax.ShapeDtypeStruct((width, units), down.dtype)] * 2
        + [jax.ShapeDtypeStruct((row.shape[1], lanes), row.dtype)],
        name="pack_down",
    )(where, down, row)


def start_loads(sems, base, pairs):
    copies = []
    for i, (source, target) in enumerate(pairs):
        copies.append(pltpu.make_async_copy(source, target, sems.at[base + i]))
        copies[-1].start()
    return copies


def normalize(raw, normed, gain_ref):
    users, features, cands = raw.shape
    chunk = 256 if features % 256 == 0 else features
    for u in range(users):

        def square(k, total):
            rows = pl.ds(pl.multiple_of(k * chunk, chunk), chunk)
            values = raw[u, rows, :].astype(jnp.float32)
            return total + jnp.sum(values * values, axis=0, keepdims=True)

        total = lax.fori_loop(0, features // chunk, square, jnp.zeros((1, cands), jnp.float32))
        scale = lax.rsqrt(total * (1.0 / features) + 1e-06)

        def apply(k, carry):
            rows = pl.ds(pl.multiple_of(k * chunk, chunk), chunk)
            values = raw[u, rows, :].astype(jnp.float32)
            normed[rows, u * cands : (u + 1) * cands] = (
                values * scale * gain_ref[rows, :]
            ).astype(jnp.bfloat16)
            return carry

        lax.fori_loop(0, features // chunk, apply, 0)


def feed_forward(where, groups, orders, gain, expand, down, hidden=None):
    count, chips = len(groups), len(groups[0])
    size, chip_width, cands = groups[0][0].shape
    features = gain.shape[0]
    weights = expand if hidden is None else down
    layers = len(weights[0])
    units = expand[0][0].shape[0] // 2
    block = features // layers
    lanes = size * cands
    expands, downs = hidden is None, down is not None
    outs = chips if orders is None else 2

    def body(where_ref, *refs):
        refs = list(refs)
        take = lambda n: [refs.pop(0) for _ in range(n)]
        chip, layer = where_ref[0], where_ref[2]
        at_chip = lambda t: pl.ds(pl.multiple_of((chip ^ t) * chip_width, chip_width), chip_width)
        at_layer = lambda s: pl.ds(pl.multiple_of((layer ^ s) * block, block), block)
        if expands:
            part_refs = take(count * chips)
            (gain_ref,) = take(1)
            expand_refs = take(2 * layers)
        else:
            (given_ref,) = take(1)
        if downs:
            down_refs = take(2 * layers)
            out_refs = take(outs * count)
            (hidden_ref,) = take(1)
        else:
            (hidden_ref,) = take(1)
        (sems,) = take(1)
        if expands:
            raw, normed, wide = take(3)
            part_loads = start_loads(
                sems,
                0,
                [
                    (part_refs[g * chips + t], raw.at[pl.ds(g * size, size), at_chip(t), :])
                    for g in range(count)
                    for t in range(chips)
                ],
            )
            expand_loads = start_loads(
                sems,
                count * chips,
                [
                    (expand_refs[i * layers + s], wide.at[i, :, at_layer(s)])
                    for i in range(2)
                    for s in range(layers)
                ],
            )
        else:
            given_loads = start_loads(sems, 0, [(given_ref, hidden_ref)])
        if downs:
            (narrow,) = take(1)
            down_loads = start_loads(
                sems,
                count * chips + 2 * layers,
                [
                    (down_refs[i * layers + s], narrow.at[at_layer(s), pl.ds(i * units, units)])
                    for i in range(2)
                    for s in range(layers)
                ],
            )
        if expands:
            for copy in part_loads:
                copy.wait()
            normalize(raw, normed, gain_ref)
            tile = tile_of(units)
            for i in range(2):
                for s in range(layers):
                    expand_loads[i * layers + s].wait()
                for f in range(0, units, tile):
                    gate = dot(wide[i, 2 * f : 2 * f + tile, :], normed[...], ((1,), (0,)))
                    upward = dot(
                        wide[i, 2 * f + tile : 2 * (f + tile), :], normed[...], ((1,), (0,))
                    )
                    hidden_ref[i * units + f : i * units + f + tile, :] = (
                        gate / (1.0 + jnp.exp(-gate)) * upward
                    ).astype(jnp.bfloat16)
        if downs:
            for copy in down_loads if expands else given_loads + down_loads:
                copy.wait()
            for g in range(count):
                for i in range(chips):
                    target = chips - 1 - i if orders is None else orders[g][i]
                    result = dot(
                        narrow[at_chip(target), :],
                        hidden_ref[:, g * lanes : (g + 1) * lanes],
                        ((1,), (0,)),
                    ).astype(jnp.bfloat16)
                    for u in range(size):
                        mine = result[:, u * cands : (u + 1) * cands]
                        if orders is None:
                            out_refs[chips * g + target][u] = mine
                        else:
                            out_refs[2 * g + (i >= chips // 2)][i % (chips // 2), u] = mine

    total = count * lanes
    hidden_shape = (2 * units, total)
    inputs, in_specs, scratch = [where], [SMEM_WHOLE], []
    if expands:
        inputs += sum(groups, []) + [gain] + expand[0] + expand[1]
        in_specs += [IN_PLACE] * (count * chips) + [VMEM_WHOLE] + [IN_PLACE] * (2 * layers)
        scratch += [
            pltpu.VMEM((count * size, features, cands), jnp.bfloat16),
            pltpu.VMEM((features, total), jnp.bfloat16),
            pltpu.VMEM((2, 2 * units, features), jnp.bfloat16),
        ]
    else:
        inputs += [hidden]
        in_specs += [IN_PLACE]
    scratch = [pltpu.SemaphoreType.DMA((count * chips + 4 * layers,))] + scratch
    if downs:
        inputs += down[0] + down[1]
        in_specs += [IN_PLACE] * (2 * layers)
        shape = (size, chip_width, cands)
        if orders is not None:
            shape = (chips // 2,) + shape
        out_shape = [jax.ShapeDtypeStruct(shape, jnp.bfloat16)] * (outs * count)
        scratch += [pltpu.VMEM((features, 2 * units), jnp.bfloat16)]
        scratch = [pltpu.VMEM(hidden_shape, jnp.bfloat16)] + scratch
    else:
        out_shape = [jax.ShapeDtypeStruct(hidden_shape, jnp.bfloat16)]
    return pl.pallas_call(
        body,
        in_specs=in_specs,
        out_specs=[VMEM_WHOLE] * len(out_shape),
        out_shape=out_shape,
        scratch_shapes=scratch,
        name="feed_forward",
    )(*inputs)


def make_shards(dp_count, mp_count):
    chips = mp_count // 2

    def across(x, t):
        return swap(x, "mp", mp_count, 2 * t)

    def beside(x):
        return swap(x, "mp", mp_count, 1)

    def to_chips(x):
        return [x] + [across(x, t) for t in range(chips - 1, 0, -1)][::-1]

    bits = [1 << i for i in range((chips - 1).bit_length())]

    def doubled(x, order):
        parts = {0: x}
        for bit in order:
            new = {bit: across(x, bit)}
            new.update({t | bit: across(part, bit) for t, part in parts.items() if t})
            parts.update(new)
        return [parts[t] for t in range(chips)]

    def block_order(order):
        blocks = [0]
        for bit in order[::-1]:
            blocks = blocks + [t | bit for t in blocks]
        return blocks

    def halved(near, far, order):
        wide = lambda x: x.astype(jnp.float32)
        near = [wide(near[i]) for i in range(chips // 2)]
        for bit in order:
            got = across(far, bit)
            near = [block + wide(got[j]) for j, block in enumerate(near)]
            count = len(near) // 2
            if count:
                far = jnp.stack(near[count:]).astype(jnp.bfloat16)
                near = near[:count]
        return near[0]

    def shards(behaviors, candidates, lengths, bilinear, norm_gain, w_gate, w_up, w_down):
        users, width, cands = candidates.shape
        features = bilinear.shape[1]
        half = users // 2
        group = half // 2
        rows = group * cands // chips
        member, layer = lax.axis_index("mp"), lax.axis_index("dp")
        core, chip = member % 2, member // 2
        far_layer = dp_count // 2
        side = layer // far_layer
        where = jnp.stack([chip, core, layer, side]).astype(jnp.int32)

        given_cands = beside(candidates)
        cand_parts = []
        for g in range(2):
            own_cands = jnp.concatenate(
                [pick(x, core * 2 + g, group, 0) for x in (candidates, given_cands)], axis=1
            )
            cand_parts.append(to_chips(own_cands))
        behavior_sides = [behaviors, beside(behaviors)]
        bilinears = [bilinear, beside(bilinear)]

        def layer_swap(x, s):
            return swap(x, "dp", dp_count, s)

        def spread(own, other):
            got = {far_layer: layer_swap(other, far_layer), 0: own}
            for s in range(1, far_layer):
                got[s] = layer_swap(own, s)
            return got

        def forward(got):
            return [
                got[s] if s in got else layer_swap(got[far_layer], s ^ far_layer)
                for s in range(dp_count)
            ]

        expand_got = spread(*pack_expand(w_gate, w_up, far_layer))
        *down_packs, gain = pack_down(where, w_down, norm_gain[None, :], cands)
        down_got = spread(*down_packs)
        parts, pooled = [], []
        for g in range(2):
            shares = score_parts(where, cand_parts[g], bilinears, behavior_sides, rows, g)
            parts.append([shares[0]] + [across(shares[t], t) for t in range(chips - 1, 0, -1)])
        expand_own = forward(expand_got)
        down_own = forward(down_got)
        for g in range(2):
            probs = softmax_rows(where, lengths, parts[g], cands, features, g)
            prob_parts = to_chips(probs)
            pooled.append(pool(where, prob_parts, behavior_sides, cands, g))
        orders = [bits, bits[::-1]]

        partner_pooled, own_parts, partner_parts = [], [], []
        for g in range(2):
            partner_pooled.append(layer_swap(pooled[g], far_layer))
            own_parts.append(doubled(pooled[g], orders[g]))
            partner_parts.append(to_chips(partner_pooled[g]))

        def besides(pieces):
            other = []
            for piece in pieces:
                other.append(beside(piece))
            return [pieces, other]

        expand = besides(expand_own)
        down = besides(down_own)
        blocks = [block_order(order) for order in orders]
        (own_hidden,) = feed_forward(where, own_parts, blocks, gain, expand, None)
        (partner_hidden,) = feed_forward(where, [partner_parts[0]], None, gain, expand, None)
        totals = []
        for g in range(2):
            shares = feed_forward(
                where, [partner_parts[g]], None, gain, expand, down, (partner_hidden, None)[g]
            )
            total = shares[0].astype(jnp.float32)
            for t in range(chips - 1, 0, -1):
                total = total + across(shares[t], t).astype(jnp.float32)
            totals.append(layer_swap(total.astype(jnp.bfloat16), far_layer))
        own_blocks = feed_forward(where, own_parts, blocks, gain, expand, down, own_hidden)
        interest = []
        for i, order in enumerate(orders):
            interest.append(
                halved(*own_blocks[2 * i : 2 * i + 2], order) + totals[i].astype(jnp.float32)
            )
        interest = jnp.concatenate(interest, axis=0).astype(jnp.bfloat16)
        kept = pick(interest, core, width, 1)
        given = beside(pick(interest, 1 - core, width, 1))
        return jnp.concatenate(
            [jnp.where(core == 0, kept, given), jnp.where(core == 0, given, kept)], axis=0
        )

    return shards


def solution(mesh):
    return jax.shard_map(
        make_shards(mesh.shape["dp"], mesh.shape["mp"]),
        mesh=mesh,
        in_specs=(
            P("dp", "mp", None),
            P("dp", "mp", None),
            P("dp"),
            P("mp", None),
            P(),
            P("dp", "mp"),
            P("dp", "mp"),
            P("mp", "dp"),
        ),
        out_specs=P("dp", "mp", None),
        check_vma=False,
    )
```

```python
import math

import jax
import jax.numpy as jnp
from jax import lax
from jax.experimental import pallas as pl
from jax.experimental.pallas import tpu as pltpu
from jax.sharding import PartitionSpec as P


VMEM_WHOLE = pl.BlockSpec(memory_space=pltpu.VMEM)
SMEM_WHOLE = pl.BlockSpec(memory_space=pltpu.SMEM)
IN_PLACE = pl.BlockSpec(memory_space=pltpu.HBM)


def pick(x, index, size, axis):
    return lax.dynamic_slice_in_dim(x, index * size, size, axis)


def swap(x, axis_name, count, offset):
    return lax.ppermute(x, axis_name, [(i, i ^ offset) for i in range(count)])


def in_vmem(arrays):
    return [pltpu.with_memory_space_constraint(x, pltpu.VMEM) for x in arrays]


def dot(a, b, dims):
    return lax.dot_general(a, b, (dims, ((), ())), preferred_element_type=jnp.float32)


def score_parts(where, cand_parts, bilinears, behaviors, rows, which):
    chips = len(cand_parts)
    group, chip_width, cands = cand_parts[0].shape
    width, features = bilinears[0].shape
    users, _, length = behaviors[0].shape
    blocks = cands // rows
    steps = group // 2

    def body(where_ref, *refs):
        cand_refs = refs[:chips]
        bilinear_refs = refs[chips : chips + 2]
        behavior_refs = refs[chips + 2 : chips + 4]
        out_refs = refs[chips + 4 :]
        chip, core = where_ref[0], where_ref[1]
        step = pl.program_id(0)
        queries = []
        for bilinear_ref in bilinear_refs:
            total = jnp.zeros((width, 2 * cands), jnp.float32)
            for t in range(chips):
                pair = jnp.concatenate([cand_refs[t][0], cand_refs[t][1]], axis=1)
                start = pl.multiple_of((chip ^ t) * chip_width, chip_width)
                if width % 128:
                    swapped = jnp.concatenate([pair[width:], pair[:width]], axis=0)
                    pair = jnp.where(core == 0, pair, swapped)
                    total += dot(bilinear_ref[:, pl.ds(start, chip_width)], pair, ((1,), (0,)))
                    continue
                for side in range(2):
                    at = pl.ds(pl.multiple_of(start + (core ^ side) * width, width), width)
                    part = pair[side * width : (side + 1) * width]
                    total += dot(bilinear_ref[:, at], part, ((1,), (0,)))
            queries.append(total.astype(jnp.bfloat16))
        for i in range(2):
            scores = jnp.zeros((cands, length), jnp.float32)
            for query, behavior_ref in zip(queries, behavior_refs):
                mine = query[:, i * cands : (i + 1) * cands]
                scores += dot(mine, behavior_ref[i], ((0,), (0,)))
            for b in range(blocks):
                target = chip ^ ((2 * step + i) * blocks + b)
                for t in range(chips):

                    @pl.when(target == t)
                    def _():
                        out_refs[t][...] = scores[b * rows : (b + 1) * rows]

    pair_block = lambda shape: pl.BlockSpec((2,) + shape, lambda i, w: (i, 0, 0))
    mine_block = lambda shape: pl.BlockSpec((2,) + shape, lambda i, w: ((w[1] * (users // 2) + which * group) // 2 + i, 0, 0))
    whole_block = lambda shape: pl.BlockSpec(shape, lambda i, w: (0, 0))
    return pl.pallas_call(
        body,
        grid_spec=pltpu.PrefetchScalarGridSpec(
            num_scalar_prefetch=1,
            grid=(steps,),
            in_specs=[pair_block((chip_width, cands))] * chips
            + [whole_block((width, features))] * 2
            + [mine_block((width, length))] * 2,
            out_specs=[whole_block((rows, length))] * chips,
        ),
        out_shape=[jax.ShapeDtypeStruct((rows, length), jnp.float32)] * chips,
        name="scores",
        compiler_params=pltpu.CompilerParams(vmem_limit_bytes=24 << 20),
    )(where, *cand_parts, *bilinears, *behaviors)


def softmax_rows(where, lengths, parts, cands, features, which):
    rows, length = parts[0].shape
    half = lengths.shape[0] // 2

    def body(where_ref, lengths_ref, *refs):
        part_refs, out_ref = refs[:-1], refs[-1]
        user = where_ref[1] * half + which * (half // 2) + where_ref[0] * rows // cands
        total = part_refs[0][...]
        for part_ref in part_refs[1:]:
            total += part_ref[...]
        scores = total * (1.0 / math.sqrt(features))
        live = lax.broadcasted_iota(jnp.int32, (rows, length), 1) < lengths_ref[user]
        masked = jnp.where(live, scores, -1e30)
        highest = jnp.max(masked, axis=-1, keepdims=True)
        expons = jnp.where(live, jnp.exp(masked - highest), 0.0)
        out_ref[...] = (expons / jnp.sum(expons, axis=-1, keepdims=True)).astype(jnp.bfloat16)

    return pl.pallas_call(
        body,
        in_specs=[SMEM_WHOLE, SMEM_WHOLE] + [VMEM_WHOLE] * len(parts),
        out_specs=VMEM_WHOLE,
        out_shape=jax.ShapeDtypeStruct((rows, length), jnp.bfloat16),
        name="softmax",
        compiler_params=pltpu.CompilerParams(vmem_limit_bytes=8 << 20),
    )(where, lengths, parts[0], *in_vmem(parts[1:]))


def pool(where, prob_parts, behaviors, cands, which):
    chips = len(prob_parts)
    rows, length = prob_parts[0].shape
    users, width, _ = behaviors[0].shape
    half = users // 2
    group = half // 2

    def body(where_ref, *refs):
        prob_refs = refs[:chips]
        own_ref, other_ref, out_ref, probs = refs[chips:]
        chip, core = where_ref[0], where_ref[1]
        step = pl.program_id(0)

        @pl.when(step == 0)
        def _():
            for t in range(chips):
                start = pl.multiple_of((chip ^ t) * rows, rows)
                probs[pl.ds(start, rows), :] = prob_refs[t][...]

        mine = probs[pl.ds(pl.multiple_of(step * cands, cands), cands), :]
        for side, ref in ((core, own_ref), (1 - core, other_ref)):
            start = pl.multiple_of(side * width, width)
            out_ref[0, pl.ds(start, width), :] = dot(ref[0], mine, ((1,), (1,))).astype(
                jnp.bfloat16
            )

    mine_block = pl.BlockSpec(
        (1, width, length), lambda i, w: (w[1] * half + which * group + i, 0, 0)
    )
    return pl.pallas_call(
        body,
        grid_spec=pltpu.PrefetchScalarGridSpec(
            num_scalar_prefetch=1,
            grid=(group,),
            in_specs=[pl.BlockSpec((rows, length), lambda i, w: (0, 0))]
            + [VMEM_WHOLE] * (chips - 1)
            + [mine_block] * 2,
            out_specs=pl.BlockSpec((1, 2 * width, cands), lambda i, w: (i, 0, 0)),
            scratch_shapes=[pltpu.VMEM((group * cands, length), jnp.bfloat16)],
        ),
        out_shape=jax.ShapeDtypeStruct((group, 2 * width, cands), jnp.bfloat16),
        name="pool",
        compiler_params=pltpu.CompilerParams(vmem_limit_bytes=16 << 20),
    )(where, prob_parts[0], *in_vmem(prob_parts[1:]), *behaviors)


def tile_of(units):
    return min(256, units)


def pack_expand(gate, up, far_layer):
    depth, units = gate.shape[0], gate.shape[1] // 2
    tile = tile_of(units)
    tiles = units // tile

    def body(gate_ref, up_ref, own_ref, other_ref, gates, ups, outs, sems):
        side = lax.axis_index("dp") // far_layer
        loads = []
        for k, which in enumerate((1, 0)):
            at = pl.ds(pl.multiple_of((side ^ which) * units, units), units)
            for i, (ref, buffer) in enumerate(((gate_ref, gates), (up_ref, ups))):
                loads.append(pltpu.make_async_copy(ref.at[:, at], buffer.at[k], sems.at[k, i]))
                loads[-1].start()
        stores = []
        for k, target in enumerate((other_ref, own_ref)):
            for i, buffer in enumerate((gates, ups)):
                loads[2 * k + i].wait()
                for f in range(tiles):
                    outs[k, (2 * f + i) * tile : (2 * f + i + 1) * tile, :] = buffer[
                        k, :, f * tile : (f + 1) * tile
                    ].T
            stores.append(pltpu.make_async_copy(outs.at[k], target, sems.at[k, 2]))
            stores[-1].start()
        for store in stores:
            store.wait()

    return pl.pallas_call(
        body,
        in_specs=[IN_PLACE] * 2,
        out_specs=[IN_PLACE] * 2,
        out_shape=[jax.ShapeDtypeStruct((2 * units, depth), gate.dtype)] * 2,
        scratch_shapes=[
            pltpu.VMEM((2, depth, units), gate.dtype),
            pltpu.VMEM((2, depth, units), gate.dtype),
            pltpu.VMEM((2, 2 * units, depth), gate.dtype),
            pltpu.SemaphoreType.DMA((2, 3)),
        ],
        name="pack_expand",
        compiler_params=pltpu.CompilerParams(vmem_limit_bytes=16 << 20),
    )(gate, up)


def pack_down(where, down, row, lanes):
    units, width = down.shape[0] // 2, down.shape[1]

    def body(where_ref, down_ref, row_ref, own_ref, other_ref, column_ref):
        for which, ref in enumerate((own_ref, other_ref)):
            start = pl.multiple_of((where_ref[3] ^ which) * units, units)
            ref[...] = down_ref[pl.ds(start, units), :].T
        column_ref[...] = jnp.broadcast_to(row_ref[...], (lanes, row.shape[1])).T

    return pl.pallas_call(
        body,
        in_specs=[SMEM_WHOLE] + [VMEM_WHOLE] * 2,
        out_specs=[VMEM_WHOLE] * 3,
        out_shape=[jax.ShapeDtypeStruct((width, units), down.dtype)] * 2
        + [jax.ShapeDtypeStruct((row.shape[1], lanes), row.dtype)],
        name="pack_down",
        compiler_params=pltpu.CompilerParams(vmem_limit_bytes=16 << 20),
    )(where, down, row)


def start_loads(sems, base, pairs):
    copies = []
    for i, (source, target) in enumerate(pairs):
        copies.append(pltpu.make_async_copy(source, target, sems.at[base + i]))
        copies[-1].start()
    return copies


def normalize(raw, normed, gain_ref):
    users, features, cands = raw.shape
    chunk = 256 if features % 256 == 0 else features
    for u in range(users):

        def square(k, total):
            rows = pl.ds(pl.multiple_of(k * chunk, chunk), chunk)
            values = raw[u, rows, :].astype(jnp.float32)
            return total + jnp.sum(values * values, axis=0, keepdims=True)

        total = lax.fori_loop(0, features // chunk, square, jnp.zeros((1, cands), jnp.float32))
        scale = lax.rsqrt(total * (1.0 / features) + 1e-06)

        def apply(k, carry):
            rows = pl.ds(pl.multiple_of(k * chunk, chunk), chunk)
            values = raw[u, rows, :].astype(jnp.float32)
            normed[rows, u * cands : (u + 1) * cands] = (
                values * scale * gain_ref[rows, :]
            ).astype(jnp.bfloat16)
            return carry

        lax.fori_loop(0, features // chunk, apply, 0)


def feed_forward(where, groups, orders, gain, expand, down, hidden=None):
    count, chips = len(groups), len(groups[0])
    size, chip_width, cands = groups[0][0].shape
    features = gain.shape[0]
    weights = expand if hidden is None else down
    layers = len(weights[0])
    units = expand[0][0].shape[0] // 2
    block = features // layers
    lanes = size * cands
    expands, downs = hidden is None, down is not None
    outs = chips if orders is None else 2

    def body(where_ref, *refs):
        refs = list(refs)
        take = lambda n: [refs.pop(0) for _ in range(n)]
        chip, layer = where_ref[0], where_ref[2]
        at_chip = lambda t: pl.ds(pl.multiple_of((chip ^ t) * chip_width, chip_width), chip_width)
        at_layer = lambda s: pl.ds(pl.multiple_of((layer ^ s) * block, block), block)
        if expands:
            part_refs = take(count * chips)
            (gain_ref,) = take(1)
            expand_refs = take(2 * layers)
        else:
            (given_ref,) = take(1)
        if downs:
            down_refs = take(2 * layers)
            out_refs = take(outs * count)
            (hidden_ref,) = take(1)
        else:
            (hidden_ref,) = take(1)
        (sems,) = take(1)
        if expands:
            raw, normed, wide = take(3)
            part_loads = start_loads(
                sems,
                0,
                [
                    (part_refs[g * chips + t], raw.at[pl.ds(g * size, size), at_chip(t), :])
                    for g in range(count)
                    for t in range(chips)
                ],
            )
            expand_loads = start_loads(
                sems,
                count * chips,
                [
                    (expand_refs[i * layers + s], wide.at[i, :, at_layer(s)])
                    for i in range(2)
                    for s in range(layers)
                ],
            )
        else:
            given_loads = start_loads(sems, 0, [(given_ref, hidden_ref)])
        if downs:
            (narrow,) = take(1)
            down_loads = start_loads(
                sems,
                count * chips + 2 * layers,
                [
                    (down_refs[i * layers + s], narrow.at[at_layer(s), pl.ds(i * units, units)])
                    for i in range(2)
                    for s in range(layers)
                ],
            )
        if expands:
            for copy in part_loads:
                copy.wait()
            normalize(raw, normed, gain_ref)
            tile = tile_of(units)
            for i in range(2):
                for s in range(layers):
                    expand_loads[i * layers + s].wait()
                for f in range(0, units, tile):
                    gate = dot(wide[i, 2 * f : 2 * f + tile, :], normed[...], ((1,), (0,)))
                    upward = dot(
                        wide[i, 2 * f + tile : 2 * (f + tile), :], normed[...], ((1,), (0,))
                    )
                    hidden_ref[i * units + f : i * units + f + tile, :] = (
                        gate / (1.0 + jnp.exp(-gate)) * upward
                    ).astype(jnp.bfloat16)
        if downs:
            for copy in down_loads if expands else given_loads + down_loads:
                copy.wait()
            for g in range(count):
                for i in range(chips):
                    target = chips - 1 - i if orders is None else orders[g][i]
                    result = dot(
                        narrow[at_chip(target), :],
                        hidden_ref[:, g * lanes : (g + 1) * lanes],
                        ((1,), (0,)),
                    ).astype(jnp.bfloat16)
                    for u in range(size):
                        mine = result[:, u * cands : (u + 1) * cands]
                        if orders is None:
                            out_refs[chips * g + target][u] = mine
                        else:
                            out_refs[2 * g + (i >= chips // 2)][i % (chips // 2), u] = mine

    total = count * lanes
    hidden_shape = (2 * units, total)
    inputs, in_specs, scratch = [where], [SMEM_WHOLE], []
    if expands:
        inputs += sum(groups, []) + [gain] + expand[0] + expand[1]
        in_specs += [IN_PLACE] * (count * chips) + [VMEM_WHOLE] + [IN_PLACE] * (2 * layers)
        scratch += [
            pltpu.VMEM((count * size, features, cands), jnp.bfloat16),
            pltpu.VMEM((features, total), jnp.bfloat16),
            pltpu.VMEM((2, 2 * units, features), jnp.bfloat16),
        ]
    else:
        inputs += [hidden]
        in_specs += [IN_PLACE]
    scratch = [pltpu.SemaphoreType.DMA((count * chips + 4 * layers,))] + scratch
    if downs:
        inputs += in_vmem(down[0] + down[1])
        in_specs += [VMEM_WHOLE] * (2 * layers)
        shape = (size, chip_width, cands)
        if orders is not None:
            shape = (chips // 2,) + shape
        out_shape = [jax.ShapeDtypeStruct(shape, jnp.bfloat16)] * (outs * count)
        scratch += [pltpu.VMEM((features, 2 * units), jnp.bfloat16)]
        scratch = [pltpu.VMEM(hidden_shape, jnp.bfloat16)] + scratch
    else:
        out_shape = [jax.ShapeDtypeStruct(hidden_shape, jnp.bfloat16)]
    return pl.pallas_call(
        body,
        in_specs=in_specs,
        out_specs=[VMEM_WHOLE] * len(out_shape),
        out_shape=out_shape,
        scratch_shapes=scratch,
        name="feed_forward",
        compiler_params=pltpu.CompilerParams(vmem_limit_bytes=36 << 20),
    )(*inputs)


def make_shards(dp_count, mp_count):
    chips = mp_count // 2

    def across(x, t):
        return swap(x, "mp", mp_count, 2 * t)

    def beside(x):
        return swap(x, "mp", mp_count, 1)

    def to_chips(x):
        return [x] + [across(x, t) for t in range(chips - 1, 0, -1)][::-1]

    bits = [1 << i for i in range((chips - 1).bit_length())]

    def doubled(x, order):
        parts = {0: x}
        for bit in order:
            new = {bit: across(x, bit)}
            new.update({t | bit: across(part, bit) for t, part in parts.items() if t})
            parts.update(new)
        return [parts[t] for t in range(chips)]

    def block_order(order):
        blocks = [0]
        for bit in order[::-1]:
            blocks = blocks + [t | bit for t in blocks]
        return blocks

    def halved(near, far, order):
        wide = lambda x: x.astype(jnp.float32)
        near = [wide(near[i]) for i in range(chips // 2)]
        for bit in order:
            got = across(far, bit)
            near = [block + wide(got[j]) for j, block in enumerate(near)]
            count = len(near) // 2
            if count:
                far = jnp.stack(near[count:]).astype(jnp.bfloat16)
                near = near[:count]
        return near[0]

    def shards(behaviors, candidates, lengths, bilinear, norm_gain, w_gate, w_up, w_down):
        users, width, cands = candidates.shape
        features = bilinear.shape[1]
        half = users // 2
        group = half // 2
        rows = group * cands // chips
        member, layer = lax.axis_index("mp"), lax.axis_index("dp")
        core, chip = member % 2, member // 2
        far_layer = dp_count // 2
        side = layer // far_layer
        where = jnp.stack([chip, core, layer, side]).astype(jnp.int32)

        given_cands = beside(candidates)
        cand_parts = []
        for g in range(2):
            own_cands = jnp.concatenate(
                [pick(x, core * 2 + g, group, 0) for x in (candidates, given_cands)], axis=1
            )
            cand_parts.append(to_chips(own_cands))
        behavior_sides = [behaviors, beside(behaviors)]
        bilinears = [bilinear, beside(bilinear)]

        def layer_swap(x, s):
            return swap(x, "dp", dp_count, s)

        def spread(own, other):
            got = {far_layer: layer_swap(other, far_layer), 0: own}
            for s in range(1, far_layer):
                got[s] = layer_swap(own, s)
            return got

        def forward(got):
            return [
                got[s] if s in got else layer_swap(got[far_layer], s ^ far_layer)
                for s in range(dp_count)
            ]

        expand_got = spread(*pack_expand(w_gate, w_up, far_layer))
        *down_packs, gain = pack_down(where, w_down, norm_gain[None, :], cands)
        down_got = spread(*down_packs)
        parts, pooled = [], []
        for g in range(2):
            shares = score_parts(where, cand_parts[g], bilinears, behavior_sides, rows, g)
            parts.append([shares[0]] + [across(shares[t], t) for t in range(chips - 1, 0, -1)])
        expand_own = forward(expand_got)
        down_own = forward(down_got)
        for g in range(2):
            probs = softmax_rows(where, lengths, parts[g], cands, features, g)
            prob_parts = to_chips(probs)
            pooled.append(pool(where, prob_parts, behavior_sides, cands, g))
        orders = [bits, bits[::-1]]

        partner_pooled, own_parts, partner_parts = [], [], []
        for g in range(2):
            partner_pooled.append(layer_swap(pooled[g], far_layer))
            own_parts.append(doubled(pooled[g], orders[g]))
            partner_parts.append(to_chips(partner_pooled[g]))

        def besides(pieces):
            other = []
            for piece in pieces:
                other.append(beside(piece))
            return [pieces, other]

        expand = besides(expand_own)
        down = besides(down_own)
        blocks = [block_order(order) for order in orders]
        (own_hidden,) = feed_forward(where, own_parts, blocks, gain, expand, None)
        (partner_hidden,) = feed_forward(where, [partner_parts[0]], None, gain, expand, None)
        totals = []
        for g in range(2):
            shares = feed_forward(
                where, [partner_parts[g]], None, gain, expand, down, (partner_hidden, None)[g]
            )
            total = shares[0].astype(jnp.float32)
            for t in range(chips - 1, 0, -1):
                total = total + across(shares[t], t).astype(jnp.float32)
            totals.append(layer_swap(total.astype(jnp.bfloat16), far_layer))
        own_blocks = feed_forward(where, own_parts, blocks, gain, expand, down, own_hidden)
        interest = []
        for i, order in enumerate(orders):
            interest.append(
                halved(*own_blocks[2 * i : 2 * i + 2], order) + totals[i].astype(jnp.float32)
            )
        interest = jnp.concatenate(interest, axis=0).astype(jnp.bfloat16)
        kept = pick(interest, core, width, 1)
        given = beside(pick(interest, 1 - core, width, 1))
        return jnp.concatenate(
            [jnp.where(core == 0, kept, given), jnp.where(core == 0, given, kept)], axis=0
        )

    return shards


def solution(mesh):
    return jax.shard_map(
        make_shards(mesh.shape["dp"], mesh.shape["mp"]),
        mesh=mesh,
        in_specs=(
            P("dp", "mp", None),
            P("dp", "mp", None),
            P("dp"),
            P("mp", None),
            P(),
            P("dp", "mp"),
            P("dp", "mp"),
            P("mp", "dp"),
        ),
        out_specs=P("dp", "mp", None),
        check_vma=False,
    )
```
